32 devices in a mesh: dp: 8 (over y, x, core), tensor: 4 (over z).
Axes of the slice: x: 2, y: 2, z: 4, core: 2. Of those that a mesh axis runs over, the one named last changes fastest.
Arguments:
- states_in: bfloat16 [8192, 1152], P(('dp', 'tensor')), may hold values from -6 to 6
- teacher: bfloat16 [8192, 1152], P(('dp', 'tensor')), may hold values from -6 to 6
- valid_counts: int32 [16], P('dp'), may hold values from 128 to 512
- attn_norm_gain: bfloat16 [1152], replicated, may hold values from 0.25 to 1.75
- attn_norm_bias: bfloat16 [1152], replicated, may hold values from -0.1875 to 0.1875
- query_weight: bfloat16 [1152, 1152], P(None, 'tensor'), may hold values from -0.1875 to 0.1875
- query_bias: bfloat16 [1152], P('tensor'), may hold values from -3 to 3
- key_weight: bfloat16 [1152, 1152], P(None, 'tensor'), may hold values from -0.1875 to 0.1875
- value_weight: bfloat16 [1152, 1152], P(None, 'tensor'), may hold values from -0.1875 to 0.1875
- value_bias: bfloat16 [1152], P('tensor'), may hold values from -0.1875 to 0.1875
- output_weight: bfloat16 [1152, 1152], P('tensor'), may hold values from -3 to 3
- output_bias: bfloat16 [1152], replicated, may hold values from -0.625 to 0.625
- mlp_norm_gain: bfloat16 [1152], replicated, may hold values from 0.25 to 1.75
- mlp_norm_bias: bfloat16 [1152], replicated, may hold values from -0.625 to 0.625
- up_weight: bfloat16 [1152, 4304], P(None, 'tensor'), may hold values from -0.1875 to 0.1875
- up_bias: bfloat16 [4304], P('tensor'), may hold values from -1.25 to 1.25
- down_weight: bfloat16 [4304, 1152], P('tensor'), may hold values from -0.09375 to 0.09375
- down_bias: bfloat16 [1152], replicated, may hold values from -0.625 to 0.625
Outputs:
- out_states: bfloat16 [8192, 1152], P(('dp', 'tensor'))
- distill_loss: float32 [], replicated
- grad_input: bfloat16 [8192, 1152], P(('dp', 'tensor'))
- grad_attn_norm_gain: float32 [1152], replicated
- grad_attn_norm_bias: float32 [1152], replicated
- grad_query_weight: float32 [1152, 1152], P(None, 'tensor')
- grad_query_bias: float32 [1152], P('tensor')
- grad_key_weight: float32 [1152, 1152], P(None, 'tensor')
- grad_value_weight: float32 [1152, 1152], P(None, 'tensor')
- grad_value_bias: float32 [1152], P('tensor')
- grad_output_weight: float32 [1152, 1152], P('tensor')
- grad_output_bias: float32 [1152], replicated
- grad_mlp_norm_gain: float32 [1152], replicated
- grad_mlp_norm_bias: float32 [1152], replicated
- grad_up_weight: float32 [1152, 4304], P(None, 'tensor')
- grad_up_bias: float32 [4304], P('tensor')
- grad_down_weight: float32 [4304, 1152], P('tensor')
- grad_down_bias: float32 [1152], replicated
The draws below stay inside these ranges and needn't reach their ends.
Inputs may be any that keep to these rules, and one draw needn't show every extreme that they name: `valid_counts`: the valid patches of an image are its first count patch slots.
All inputs are finite; a program needn't handle non-finite values.
Results may differ from the reference program's by a relative error of at most 0.012.
The reference program's roundings to bfloat16 on the way count: a program that leaves them out, or rounds other values in their place, can miss the bound.
Values may be sent and summed in bfloat16 or wider, within the bound.
No kernel may reach another device: no remote copies, remote signals or barrier semaphores. Data moves between devices by JAX's collectives and lax.ppermute only.
A program may use at most 128 MiB of HBM per device.

```python
import math
import jax
import jax.numpy as jnp
from jax import lax

D = 1152
HEADS = 16
HEAD_DIM = 72
FF = 4304
SEQ = 512
IMAGES = 16
TOKENS = 8192


def set_ends(drawn, rng, smallest, top_value):
    extent = drawn.shape
    index_at = [jax.random.randint(jax.random.fold_in(rng, axis), (), 0, extent[axis]) for axis in range(len(extent))]
    drawn = drawn.at[tuple(index_at)].set(smallest)
    longest = extent.index(max(extent))
    index_at[longest] = (index_at[longest] + 1) % extent[longest]
    return drawn.at[tuple(index_at)].set(top_value)


def block_levels(rng, shape, cuts, least, high):
    def one(position, parts):
        steps = jax.random.uniform(jax.random.fold_in(jax.random.fold_in(rng, 6), position), (parts,), jnp.float32, least / len(cuts), high / len(cuts))
        return jnp.repeat(jnp.exp(steps), shape[position] // parts).reshape((-1,) + (1,) * (len(shape) - position - 1))

    level = one(*cuts[0])
    for cut in cuts[1:]:
        level = level * one(*cut)
    return level


def bell_draw(own_key, dims, scale, bound, cuts=(), held_as=jnp.bfloat16):
    factor_of = block_levels(own_key, dims, cuts, -0.22, 0.18) if cuts else 1.0
    array = jax.random.normal(own_key, dims, jnp.float32) * scale * factor_of
    return jnp.minimum(jnp.maximum(array, -bound), bound).astype(held_as)


def setup_inputs(seed: int = 0) -> dict:
    seeds = jax.random.split(jax.random.key(seed), 19)
    states_in = bell_draw(seeds[0], (TOKENS, D), 1.0, 6.0, ((0, 32),))
    teacher = bell_draw(seeds[1], (TOKENS, D), 1.0, 6.0, ((0, 32),))
    valid_counts = set_ends(jax.random.randint(seeds[2], (IMAGES,), SEQ // 4, SEQ + 1), jax.random.fold_in(seeds[2], 1), SEQ // 4, SEQ).astype(jnp.int32)
    attn_norm_gain = jnp.clip(1.0 + 0.15 * jax.random.normal(seeds[3], (D,), jnp.float32), 0.25, 1.75).astype(jnp.bfloat16)
    attn_norm_bias = bell_draw(seeds[4], (D,), 0.03, 0.1875)
    query_weight = bell_draw(seeds[5], (D, D), D ** -0.5, 0.1875, ((1, 4),))
    query_bias = bell_draw(seeds[6], (D,), 0.5, 3.0, ((0, 4),))
    key_weight = bell_draw(seeds[7], (D, D), D ** -0.5, 0.1875, ((1, 4),))
    value_weight = bell_draw(seeds[8], (D, D), D ** -0.5, 0.1875, ((1, 4),))
    value_bias = bell_draw(seeds[9], (D,), 0.03, 0.1875, ((0, 4),))
    output_weight = bell_draw(seeds[10], (D, D), (max(2 * D // SEQ, 1)) ** -0.5, 3.0, ((0, 4),))
    output_bias = bell_draw(seeds[11], (D,), 0.1, 0.625)
    mlp_norm_gain = jnp.clip(1.0 + 0.15 * jax.random.normal(seeds[12], (D,), jnp.float32), 0.25, 1.75).astype(jnp.bfloat16)
    mlp_norm_bias = bell_draw(seeds[13], (D,), 0.1, 0.625)
    up_weight = bell_draw(seeds[14], (D, FF), D ** -0.5, 0.1875, ((1, 4),))
    up_bias = bell_draw(seeds[15], (FF,), 0.2, 1.25, ((0, 4),))
    down_weight = bell_draw(seeds[16], (FF, D), FF ** -0.5, 0.09375, ((0, 4),))
    down_bias = bell_draw(seeds[17], (D,), 0.1, 0.625)
    return dict(states_in=states_in, teacher=teacher, valid_counts=valid_counts, attn_norm_gain=attn_norm_gain, attn_norm_bias=attn_norm_bias, query_weight=query_weight, query_bias=query_bias, key_weight=key_weight, value_weight=value_weight, value_bias=value_bias, output_weight=output_weight, output_bias=output_bias, mlp_norm_gain=mlp_norm_gain, mlp_norm_bias=mlp_norm_bias, up_weight=up_weight, up_bias=up_bias, down_weight=down_weight, down_bias=down_bias)


@jax.custom_vjp
def low(v):
    return lax.optimization_barrier(v.astype(jnp.bfloat16)).astype(jnp.float32)

@jax.custom_vjp
def low_back(v):
    return v

def low_keep(v):
    return (low(v), None)

def low_pass(kept, grad):
    return (grad,)

def back_keep(v):
    return (v, None)

def back_low(kept, grad):
    return (low(grad),)
low.defvjp(low_keep, low_pass)
low_back.defvjp(back_keep, back_low)

def matmul_high(left, right):
    return jnp.dot(left, right, precision=lax.Precision.HIGHEST)

def layer_norm(values, gain, bias):
    centre = lax.optimization_barrier(jnp.mean(values, axis=-1, keepdims=True))
    shifted = values - centre
    spread = lax.optimization_barrier(jnp.mean(shifted * shifted, axis=-1, keepdims=True))
    return shifted * lax.rsqrt(spread + 1e-06) * gain + bias

def image_layer(params, inputs, targets, count_valid):
    gain_one, bias_one, wquery, bquery, wkey, wvalue, bvalue, wout, bout, gain_two, bias_two, wup, bup, wdown, bdown = params
    alive = jnp.arange(SEQ, dtype=jnp.int32) < count_valid
    ln_one = low(layer_norm(inputs, gain_one, bias_one))
    query = low(low_back(matmul_high(ln_one, wquery) + bquery)).reshape(SEQ, HEADS, HEAD_DIM)
    keys = low(low_back(matmul_high(ln_one, wkey))).reshape(SEQ, HEADS, HEAD_DIM)
    values = low(low_back(matmul_high(ln_one, wvalue) + bvalue)).reshape(SEQ, HEADS, HEAD_DIM)
    scores = jnp.einsum('qhd,khd->hqk', query, keys, precision=lax.Precision.HIGHEST) * (1.0 / math.sqrt(HEAD_DIM))
    scores = low_back(scores)
    scores = jnp.where(alive[None, None, :], scores, -1e+30)
    top = lax.optimization_barrier(jnp.max(scores, axis=-1, keepdims=True))
    exps = jnp.exp(scores - top)
    probs = exps / lax.optimization_barrier(jnp.sum(exps, axis=-1, keepdims=True))
    context = jnp.einsum('hqk,khd->qhd', low(probs), values, precision=lax.Precision.HIGHEST).reshape(SEQ, D)
    context = low(low_back(context))
    hidden_one = inputs + low_back(matmul_high(context, wout)) + bout
    ln_two = low(layer_norm(hidden_one, gain_two, bias_two))
    pre_act = low_back(matmul_high(ln_two, wup) + bup)
    activ = low(jax.nn.gelu(pre_act, approximate=True))
    hidden_two = hidden_one + low_back(matmul_high(activ, wdown)) + bdown
    error_rows = (hidden_two - targets) * alive.astype(jnp.float32)[:, None]
    return (hidden_two, jnp.sum(error_rows * error_rows))

def reference(states_in, teacher, valid_counts, attn_norm_gain, attn_norm_bias, query_weight, query_bias, key_weight, value_weight, value_bias, output_weight, output_bias, mlp_norm_gain, mlp_norm_bias, up_weight, up_bias, down_weight, down_bias):
    params = (attn_norm_gain.astype(jnp.float32), attn_norm_bias.astype(jnp.float32), query_weight.astype(jnp.float32), query_bias.astype(jnp.float32), key_weight.astype(jnp.float32), value_weight.astype(jnp.float32), value_bias.astype(jnp.float32), output_weight.astype(jnp.float32), output_bias.astype(jnp.float32), mlp_norm_gain.astype(jnp.float32), mlp_norm_bias.astype(jnp.float32), up_weight.astype(jnp.float32), up_bias.astype(jnp.float32), down_weight.astype(jnp.float32), down_bias.astype(jnp.float32))
    inputs = states_in.astype(jnp.float32).reshape(IMAGES, SEQ, D)
    targets = teacher.astype(jnp.float32).reshape(IMAGES, SEQ, D)
    counts = valid_counts.astype(jnp.int32)
    token_total = jnp.sum(counts).astype(jnp.float32)
    checked_layer = jax.checkpoint(image_layer)

    def forward(weights, states):

        def step(carry, item):
            state_block, target_block, count_valid = item
            hidden_two, squares = checked_layer(weights, state_block, target_block, count_valid)
            return (carry + squares, hidden_two)
        squares_total, hidden_all = lax.scan(step, jnp.zeros((), jnp.float32), (states, targets, counts))
        return (hidden_all, squares_total)
    (hidden_all, squares_total), backward = jax.vjp(forward, params, inputs)
    loss_cotangent = jnp.ones((), jnp.float32) / token_total
    grads, grad_states = backward((jnp.zeros_like(hidden_all), loss_cotangent))
    return (hidden_all.reshape(IMAGES * SEQ, D).astype(jnp.bfloat16), squares_total / token_total, grad_states.reshape(IMAGES * SEQ, D).astype(jnp.bfloat16), grads[0], grads[1], grads[2], grads[3], grads[4], grads[5], grads[6], grads[7], grads[8], grads[9], grads[10], grads[11], grads[12], grads[13], grads[14])
```

```python
import math

import jax
import jax.numpy as jnp
from jax import lax
from jax.sharding import PartitionSpec as P

HEAD_DIM = 72


def layer_norm(values, gain, bias):
    centre = jnp.mean(values, axis=-1, keepdims=True)
    shifted = values - centre
    spread = jnp.mean(shifted * shifted, axis=-1, keepdims=True)
    return shifted * lax.rsqrt(spread + 1e-06) * gain + bias


def gelu_tanh(values):
    return jax.nn.gelu(values, approximate=True)


def times_transpose(left, right):
    return lax.dot_general(
        left, right, (((1,), (1,)), ((), ())), preferred_element_type=jnp.float32
    )


def transpose_times(left, right):
    return lax.dot_general(
        left, right, (((0,), (0,)), ((), ())), preferred_element_type=jnp.float32
    )


def exchange(value, axis, flip):
    size = lax.axis_size(axis)
    return lax.ppermute(value, axis, [(index, index ^ flip) for index in range(size)])


def gather_parts(value, axis):
    return [value] + [exchange(value, axis, flip) for flip in range(1, lax.axis_size(axis))]


def scatter_sum(parts, axis):
    total = parts[0]
    for flip in range(len(parts) - 1, 0, -1):
        total = total + exchange(parts[flip].astype(jnp.bfloat16), axis, flip).astype(jnp.float32)
    return total


def butterfly(value, axis):
    flip = 1
    while flip < lax.axis_size(axis):
        value = value + exchange(value, axis, flip)
        flip *= 2
    return value


def split_heads(block):
    return block.reshape(block.shape[0], -1, HEAD_DIM)


def masked_scores(query_view, key_view, key_alive, score_scale):
    scores = (
        jnp.einsum("qhd,khd->hqk", query_view, key_view, preferred_element_type=jnp.float32)
        * score_scale
    )
    return jnp.where(key_alive[None, None, :], scores, -1e30)


def per_device(
    states_in,
    teacher,
    valid_counts,
    attn_norm_gain,
    attn_norm_bias,
    query_weight,
    query_bias,
    key_weight,
    value_weight,
    value_bias,
    output_weight,
    output_bias,
    mlp_norm_gain,
    mlp_norm_bias,
    up_weight,
    up_bias,
    down_weight,
    down_bias,
):
    f32, bf16 = jnp.float32, jnp.bfloat16
    rows = states_in.shape[0]
    tensor_size = lax.axis_size("tensor")
    image_count = valid_counts.shape[0]
    seq_len = rows * tensor_size // image_count
    share = seq_len // rows
    score_scale = 1.0 / math.sqrt(HEAD_DIM)
    here = lax.axis_index("tensor")
    image_base = here // share
    limits = []
    for image_index in range(image_count):
        picks = jnp.arange(image_count, dtype=jnp.int32) == (image_base ^ image_index)
        limits.append(jnp.sum(jnp.where(picks, valid_counts, 0)))
    alive = []
    for image_index in range(image_count):
        places = [
            ((here ^ flip) % share) * rows + jnp.arange(rows, dtype=jnp.int32)
            for flip in range(share)
        ]
        alive.append(jnp.concatenate(places) < limits[image_index])
    row_valid = alive[0][:rows].astype(f32)
    token_total = butterfly(jnp.sum(valid_counts).reshape(1, 1), "dp").astype(f32)[0, 0]
    gain_one = attn_norm_gain.astype(f32)
    bias_one = attn_norm_bias.astype(f32)
    gain_two = mlp_norm_gain.astype(f32)
    bias_two = mlp_norm_bias.astype(f32)
    states_f = states_in.astype(f32)
    ln_one, norm_one_back = jax.vjp(layer_norm, states_f, gain_one, bias_one)
    ln_one_parts = gather_parts(ln_one.astype(bf16), "tensor")
    ln_one_img = [
        jnp.concatenate(ln_one_parts[i * share : (i + 1) * share], axis=0)
        for i in range(image_count)
    ]
    saved = []
    context_list = []
    for i in range(image_count):
        query = (
            jnp.dot(ln_one_img[i], query_weight, preferred_element_type=f32)
            + query_bias.astype(f32)
        ).astype(bf16)
        keys = jnp.dot(ln_one_img[i], key_weight, preferred_element_type=f32).astype(bf16)
        values = (
            jnp.dot(ln_one_img[i], value_weight, preferred_element_type=f32)
            + value_bias.astype(f32)
        ).astype(bf16)
        query_view, key_view, value_view = split_heads(query), split_heads(keys), split_heads(values)
        scores = masked_scores(query_view, key_view, alive[i], score_scale)
        top = jnp.max(scores, axis=-1, keepdims=True)
        exps = jnp.exp(scores - top)
        totals = jnp.sum(exps, axis=-1, keepdims=True)
        probs = exps / totals
        mixed = jnp.einsum(
            "hqk,khd->qhd", probs.astype(bf16), value_view, preferred_element_type=f32
        )
        context_list.append(mixed.reshape(seq_len, -1).astype(bf16))
        saved.append((query_view, key_view, value_view, top + jnp.log(totals)))
    attn_parts = []
    for i in range(image_count):
        partial = jnp.dot(context_list[i], output_weight, preferred_element_type=f32)
        attn_parts += [partial[s * rows : (s + 1) * rows] for s in range(share)]
    attn_out = scatter_sum(attn_parts, "tensor")
    hidden_one = states_f + attn_out + output_bias.astype(f32)
    ln_two, norm_two_back = jax.vjp(layer_norm, hidden_one, gain_two, bias_two)
    ln_two_all = jnp.concatenate(gather_parts(ln_two.astype(bf16), "tensor"), axis=0)
    pre_act = jnp.dot(ln_two_all, up_weight, preferred_element_type=f32) + up_bias.astype(f32)
    activ_f, gelu_back = jax.vjp(gelu_tanh, pre_act)
    activ = activ_f.astype(bf16)
    mlp_partial = jnp.dot(activ, down_weight, preferred_element_type=f32)
    mlp_out = scatter_sum(
        [mlp_partial[s * rows : (s + 1) * rows] for s in range(tensor_size)], "tensor"
    )
    hidden_two = hidden_one + mlp_out + down_bias.astype(f32)
    out_states = hidden_two.astype(bf16)
    error_rows = (hidden_two - teacher.astype(f32)) * row_valid[:, None]
    squares_here = jnp.sum(error_rows * error_rows)
    grad_two = error_rows * (2.0 / token_total)
    cot_two = jnp.concatenate(gather_parts(grad_two.astype(bf16), "tensor"), axis=0)
    grad_down = transpose_times(activ, cot_two)
    grad_down_bias = jnp.sum(grad_two, axis=0)
    grad_activ = times_transpose(cot_two, down_weight)
    grad_pre = gelu_back(grad_activ)[0].astype(bf16)
    grad_up = transpose_times(grad_pre, ln_two_all)
    grad_up_bias = jnp.sum(grad_pre.astype(f32), axis=0)
    gln_partial = times_transpose(grad_pre, up_weight)
    grad_ln_two = scatter_sum(
        [gln_partial[s * rows : (s + 1) * rows] for s in range(tensor_size)], "tensor"
    )
    mlp_grads = lax.psum((grad_down.astype(bf16), grad_up.astype(bf16)), "dp")
    grad_hidden, grad_gain_two, grad_bias_two = norm_two_back(grad_ln_two)
    grad_one = grad_two + grad_hidden
    cot_parts = gather_parts(grad_one.astype(bf16), "tensor")
    grad_out_bias = jnp.sum(grad_one, axis=0)
    grad_qkv = [[], [], []]
    cot_img = [
        jnp.concatenate(cot_parts[i * share : (i + 1) * share], axis=0)
        for i in range(image_count)
    ]
    for i in range(image_count):
        query_view, key_view, value_view, logsum = saved[i]
        grad_view = split_heads(times_transpose(cot_img[i], output_weight).astype(bf16))
        scores = masked_scores(query_view, key_view, alive[i], score_scale)
        probs = jnp.exp(scores - logsum)
        grad_probs = jnp.einsum("qhd,khd->hqk", grad_view, value_view, preferred_element_type=f32)
        grad_value_view = jnp.einsum(
            "hqk,qhd->khd", probs.astype(bf16), grad_view, preferred_element_type=f32
        )
        inner = jnp.sum(grad_probs * probs, axis=-1, keepdims=True)
        grad_scores = (probs * (grad_probs - inner)).astype(bf16)
        grad_query_view = (
            jnp.einsum("hqk,khd->qhd", grad_scores, key_view, preferred_element_type=f32)
            * score_scale
        )
        grad_key_view = (
            jnp.einsum("hqk,qhd->khd", grad_scores, query_view, preferred_element_type=f32)
            * score_scale
        )
        for slot, piece in enumerate((grad_query_view, grad_key_view, grad_value_view)):
            grad_qkv[slot].append(piece.reshape(seq_len, -1).astype(bf16))
    back_parts = []
    for i in range(image_count):
        partial = (
            times_transpose(grad_qkv[0][i], query_weight)
            + times_transpose(grad_qkv[1][i], key_weight)
            + times_transpose(grad_qkv[2][i], value_weight)
        )
        back_parts += [partial[s * rows : (s + 1) * rows] for s in range(share)]
    grad_ln_one = scatter_sum(back_parts, "tensor")
    context = jnp.concatenate(context_list, axis=0)
    cot_one = jnp.concatenate(cot_img, axis=0)
    ln_one_all = jnp.concatenate(ln_one_img, axis=0)
    grad_query_all, grad_key_all, grad_value_all = (jnp.concatenate(p, axis=0) for p in grad_qkv)
    grad_out = transpose_times(context, cot_one)
    grad_query = transpose_times(grad_query_all, ln_one_all)
    grad_key = transpose_times(grad_key_all, ln_one_all)
    grad_value = transpose_times(grad_value_all, ln_one_all)
    attn_grads = lax.psum(
        tuple(g.astype(bf16) for g in (grad_query, grad_key, grad_value, grad_out)), "dp"
    )
    grad_states, grad_gain_one, grad_bias_one = norm_one_back(grad_ln_one)
    grad_input = (grad_one + grad_states).astype(bf16)
    by_unit = lax.psum(
        (
            jnp.sum(grad_query_all.astype(f32), axis=0),
            jnp.sum(grad_value_all.astype(f32), axis=0),
            grad_up_bias,
        ),
        "dp",
    )
    summed = lax.psum(
        (
            grad_gain_one,
            grad_bias_one,
            grad_out_bias,
            grad_gain_two,
            grad_bias_two,
            grad_down_bias,
            squares_here,
        ),
        ("dp", "tensor"),
    )
    return (
        out_states,
        summed[6] / token_total,
        grad_input,
        summed[0],
        summed[1],
        attn_grads[0].T.astype(f32),
        by_unit[0],
        attn_grads[1].T.astype(f32),
        attn_grads[2].T.astype(f32),
        by_unit[1],
        attn_grads[3].astype(f32),
        summed[2],
        summed[3],
        summed[4],
        mlp_grads[1].T.astype(f32),
        by_unit[2],
        mlp_grads[0].astype(f32),
        summed[5],
    )


def solution(mesh):
    placed = (
        P(("dp", "tensor"), None),
        P(("dp", "tensor"), None),
        P("dp"),
        P(),
        P(),
        P(None, "tensor"),
        P("tensor"),
        P(None, "tensor"),
        P(None, "tensor"),
        P("tensor"),
        P("tensor", None),
        P(),
        P(),
        P(),
        P(None, "tensor"),
        P("tensor"),
        P("tensor", None),
        P(),
    )
    return jax.shard_map(
        per_device,
        mesh=mesh,
        in_specs=placed,
        out_specs=(
            P(("dp", "tensor"), None),
            P(),
            P(("dp", "tensor"), None),
            P(),
            P(),
            P(None, "tensor"),
            P("tensor"),
            P(None, "tensor"),
            P(None, "tensor"),
            P("tensor"),
            P("tensor", None),
            P(),
            P(),
            P(),
            P(None, "tensor"),
            P("tensor"),
            P("tensor", None),
            P(),
        ),
        check_vma=False,
    )
```

```python
import math

import jax
import jax.numpy as jnp
from jax import lax
from jax.sharding import PartitionSpec as P

HEAD_DIM = 72


def layer_norm(values, gain, bias):
    centre = jnp.mean(values, axis=-1, keepdims=True)
    shifted = values - centre
    spread = jnp.mean(shifted * shifted, axis=-1, keepdims=True)
    return shifted * lax.rsqrt(spread + 1e-06) * gain + bias


def gelu_tanh(values):
    return jax.nn.gelu(values, approximate=True)


def times_transpose(left, right):
    return lax.dot_general(
        left, right, (((1,), (1,)), ((), ())), preferred_element_type=jnp.float32
    )


def transpose_times(left, right):
    return lax.dot_general(
        left, right, (((0,), (0,)), ((), ())), preferred_element_type=jnp.float32
    )


def exchange(value, axis, flip):
    size = lax.axis_size(axis)
    return lax.ppermute(value, axis, [(index, index ^ flip) for index in range(size)])


def gather_parts(value, axis):
    return [value] + [exchange(value, axis, flip) for flip in range(1, lax.axis_size(axis))]


def scatter_sum(parts, axis):
    total = parts[0]
    for flip in range(len(parts) - 1, 0, -1):
        total = total + exchange(parts[flip].astype(jnp.bfloat16), axis, flip).astype(jnp.float32)
    return total


def butterfly(value, axis):
    flip = 1
    while flip < lax.axis_size(axis):
        value = value + exchange(value, axis, flip)
        flip *= 2
    return value


class UnitPlan:
    def __init__(self, units):
        self.units = units
        self.dp = lax.axis_size("dp")
        self.tensor = lax.axis_size("tensor")
        self.rows = -(-units // (8 * self.dp)) * 8
        first = (self.rows + 15) // 16 * 8
        self.colours = [(0, first), (first, self.rows - first)]
        self.me = lax.axis_index("dp")
        self.here = lax.axis_index("tensor")
        bits = [1 << k for k in range(1, self.dp.bit_length() - 1)]
        swapped = list(bits)
        for k in range(0, len(bits) - 1, 2):
            swapped[k], swapped[k + 1] = swapped[k + 1], swapped[k]
        self.steps = [bits, swapped]

    def order(self, colour):
        order = [0]
        for flip in self.steps[colour]:
            order = order + [flip ^ seen for seen in order]
        return order

    def piece(self, padded, flip):
        return lax.dynamic_slice_in_dim(padded, (self.me ^ flip) * self.rows, self.rows, axis=0)

    def pad(self, block):
        short = self.dp * self.rows - self.units
        return jnp.pad(block, ((0, short),) + ((0, 0),) * (block.ndim - 1))

    def index_rows(self):
        listed = []
        for colour, (first, count) in enumerate(self.colours):
            for half in (0, 1):
                order = [half ^ seen for seen in self.order(colour)]
                listed += [(z, e, first, count) for e in order for z in range(1, self.tensor)]
                listed += [(0, e, first, count) for e in order]
        return listed

    def regions(self):
        start, listed = 0, []
        for _, count in self.colours:
            size = self.dp // 2 * self.tensor * count
            listed.append((start, start + size, start + 2 * size))
            start += 2 * size
        return listed

    def natural(self, vector):
        pieces, start = {}, 0
        for z, e, first, count in self.index_rows():
            pieces[z, e, first] = vector[start : start + count]
            start += count
        table = jnp.stack(
            [
                jnp.concatenate([pieces[z, e, first] for first, _ in self.colours])
                for z in range(self.tensor)
                for e in range(self.dp)
            ]
        )
        table = xor_rows(table.reshape(self.tensor, self.dp * self.rows), self.here)
        table = table.reshape(self.tensor * self.dp, self.rows)
        table = xor_rows(table, self.me)
        return table.reshape(self.tensor, self.dp * self.rows)[:, : self.units]

    def arrange(self, table):
        table = xor_rows(table.reshape(self.tensor * self.dp, self.rows), self.me)
        table = table.reshape(self.tensor, self.dp, self.rows)
        return jnp.concatenate(
            [table[z, e, first : first + count] for z, e, first, count in self.index_rows()]
        )


def xor_rows(table, amount):
    rows = jnp.arange(table.shape[0], dtype=jnp.int32)
    picks = (rows[:, None] ^ amount) == rows[None, :]
    return jnp.dot(picks.astype(jnp.float32), table, precision=lax.Precision.HIGHEST)


def gather_units(plan, block, after):
    padded = plan.pad(block)
    mine, _ = lax.optimization_barrier((plan.piece(padded, 0), after))
    foreign = [exchange(mine, "tensor", flip) for flip in range(1, plan.tensor)]
    regions = []
    for colour, (first, count) in enumerate(plan.colours):
        base = jnp.concatenate([part[first : first + count] for part in foreign], axis=0)
        for flip in plan.steps[colour]:
            base = jnp.concatenate([base, exchange(base, "dp", flip)], axis=0)
        for half, held in ((0, base), (1, exchange(base, "dp", 1))):
            regions.append(held)
            for seen in plan.order(colour):
                own = plan.piece(padded, half ^ seen)
                regions.append(own[first : first + count])
    return jnp.concatenate(regions, axis=0)


def reduce_units(plan, left, right):
    f32, bf16 = jnp.float32, jnp.bfloat16
    owned = []
    for (start, middle, end), (first, count), steps in zip(
        plan.regions(), plan.colours, plan.steps
    ):
        message = jnp.dot(left[middle:end], right, preferred_element_type=f32).astype(bf16)
        total = jnp.dot(left[start:middle], right, preferred_element_type=f32)
        total = total + exchange(message, "dp", 1).astype(f32)
        blocks = plan.dp // 2
        for flip in reversed(steps):
            blocks //= 2
            near = blocks * (plan.tensor - 1) * count
            own = 2 * near
            low = [total[:near], total[own : own + blocks * count]]
            high = [total[near:own], total[own + blocks * count :]]
            message = jnp.concatenate(high, axis=0).astype(bf16)
            total = jnp.concatenate(low, axis=0) + exchange(message, "dp", flip).astype(f32)
        owned.append([total[k * count : (k + 1) * count] for k in range(plan.tensor)])
    parts = [jnp.concatenate([colour[k] for colour in owned], axis=0) for k in range(plan.tensor)]
    return scatter_sum([parts[-1]] + parts[:-1], "tensor")


def split_heads(block):
    return block.reshape(block.shape[0], -1, HEAD_DIM)


def masked_scores(query_view, key_view, key_alive, score_scale):
    scores = (
        jnp.einsum("qhd,khd->hqk", query_view, key_view, preferred_element_type=jnp.float32)
        * score_scale
    )
    return jnp.where(key_alive[None, None, :], scores, -1e30)


def per_device(
    states_in,
    teacher,
    valid_counts,
    attn_norm_gain,
    attn_norm_bias,
    query_weight,
    query_bias,
    key_weight,
    value_weight,
    value_bias,
    output_weight,
    output_bias,
    mlp_norm_gain,
    mlp_norm_bias,
    up_weight,
    up_bias,
    down_weight,
    down_bias,
):
    f32, bf16 = jnp.float32, jnp.bfloat16
    rows = states_in.shape[0]
    tensor_size = lax.axis_size("tensor")
    image_count = valid_counts.shape[0]
    seq_len = rows * tensor_size // image_count
    share = seq_len // rows
    score_scale = 1.0 / math.sqrt(HEAD_DIM)
    here = lax.axis_index("tensor")
    image_base = here // share
    limits = []
    for image_index in range(image_count):
        picks = jnp.arange(image_count, dtype=jnp.int32) == (image_base ^ image_index)
        limits.append(jnp.sum(jnp.where(picks, valid_counts, 0)))
    alive = []
    for image_index in range(image_count):
        places = [
            ((here ^ flip) % share) * rows + jnp.arange(rows, dtype=jnp.int32)
            for flip in range(share)
        ]
        alive.append(jnp.concatenate(places) < limits[image_index])
    row_valid = alive[0][:rows].astype(f32)
    token_total = butterfly(jnp.sum(valid_counts).reshape(1, 1), "dp").astype(f32)[0, 0]
    gain_one = attn_norm_gain.astype(f32)
    bias_one = attn_norm_bias.astype(f32)
    gain_two = mlp_norm_gain.astype(f32)
    bias_two = mlp_norm_bias.astype(f32)
    states_f = states_in.astype(f32)
    ln_one, norm_one_back = jax.vjp(layer_norm, states_f, gain_one, bias_one)
    ln_one_parts = gather_parts(ln_one.astype(bf16), "tensor")
    plan = UnitPlan(up_weight.shape[1])
    last_part = ln_one_parts[-1]
    bias_parts = gather_parts(plan.pad(up_bias.astype(f32)).reshape(1, -1), "tensor")
    bias_full = plan.arrange(jnp.concatenate(bias_parts, axis=0))
    up_full = gather_units(plan, up_weight.T, last_part)
    down_full = gather_units(plan, down_weight, last_part)
    ln_one_img = [
        jnp.concatenate(ln_one_parts[i * share : (i + 1) * share], axis=0)
        for i in range(image_count)
    ]
    saved = []
    context_list = []
    for i in range(image_count):
        query = (
            jnp.dot(ln_one_img[i], query_weight, preferred_element_type=f32)
            + query_bias.astype(f32)
        ).astype(bf16)
        keys = jnp.dot(ln_one_img[i], key_weight, preferred_element_type=f32).astype(bf16)
        values = (
            jnp.dot(ln_one_img[i], value_weight, preferred_element_type=f32)
            + value_bias.astype(f32)
        ).astype(bf16)
        query_view, key_view, value_view = split_heads(query), split_heads(keys), split_heads(values)
        scores = masked_scores(query_view, key_view, alive[i], score_scale)
        top = jnp.max(scores, axis=-1, keepdims=True)
        exps = jnp.exp(scores - top)
        totals = jnp.sum(exps, axis=-1, keepdims=True)
        probs = exps / totals
        mixed = jnp.einsum(
            "hqk,khd->qhd", probs.astype(bf16), value_view, preferred_element_type=f32
        )
        context_list.append(mixed.reshape(seq_len, -1).astype(bf16))
        saved.append((query_view, key_view, value_view, top + jnp.log(totals)))
    attn_parts = []
    for i in range(image_count):
        partial = jnp.dot(context_list[i], output_weight, preferred_element_type=f32)
        attn_parts += [partial[s * rows : (s + 1) * rows] for s in range(share)]
    attn_out = scatter_sum(attn_parts, "tensor")
    hidden_one = states_f + attn_out + output_bias.astype(f32)
    ln_two, norm_two_back = jax.vjp(layer_norm, hidden_one, gain_two, bias_two)
    ln_two_low = ln_two.astype(bf16)
    pre_act = times_transpose(up_full, ln_two_low) + bias_full[:, None]
    activ_f, gelu_back = jax.vjp(gelu_tanh, pre_act)
    activ = activ_f.astype(bf16)
    mlp_out = transpose_times(activ, down_full)
    hidden_two = hidden_one + mlp_out + down_bias.astype(f32)
    out_states = hidden_two.astype(bf16)
    error_rows = (hidden_two - teacher.astype(f32)) * row_valid[:, None]
    squares_here = jnp.sum(error_rows * error_rows)
    grad_two = error_rows * (2.0 / token_total)
    cot_two = grad_two.astype(bf16)
    grad_down_own = reduce_units(plan, activ, cot_two)
    grad_down_bias = jnp.sum(grad_two, axis=0)
    grad_activ = times_transpose(down_full, cot_two)
    grad_pre = gelu_back(grad_activ)[0].astype(bf16)
    grad_up_own = reduce_units(plan, grad_pre, ln_two_low)
    grad_up_bias_all = plan.natural(jnp.sum(grad_pre.astype(f32), axis=1))
    grad_ln_two = transpose_times(grad_pre, up_full)
    mlp_grads = [
        lax.all_gather(own.astype(bf16), "dp", axis=0, tiled=True)[: plan.units]
        for own in (grad_down_own, grad_up_own)
    ]
    grad_hidden, grad_gain_two, grad_bias_two = norm_two_back(grad_ln_two)
    grad_one = grad_two + grad_hidden
    cot_parts = gather_parts(grad_one.astype(bf16), "tensor")
    grad_out_bias = jnp.sum(grad_one, axis=0)
    grad_qkv = [[], [], []]
    cot_img = [
        jnp.concatenate(cot_parts[i * share : (i + 1) * share], axis=0)
        for i in range(image_count)
    ]
    for i in range(image_count):
        query_view, key_view, value_view, logsum = saved[i]
        grad_view = split_heads(times_transpose(cot_img[i], output_weight).astype(bf16))
        scores = masked_scores(query_view, key_view, alive[i], score_scale)
        probs = jnp.exp(scores - logsum)
        grad_probs = jnp.einsum("qhd,khd->hqk", grad_view, value_view, preferred_element_type=f32)
        grad_value_view = jnp.einsum(
            "hqk,qhd->khd", probs.astype(bf16), grad_view, preferred_element_type=f32
        )
        inner = jnp.sum(grad_probs * probs, axis=-1, keepdims=True)
        grad_scores = (probs * (grad_probs - inner)).astype(bf16)
        grad_query_view = (
            jnp.einsum("hqk,khd->qhd", grad_scores, key_view, preferred_element_type=f32)
            * score_scale
        )
        grad_key_view = (
            jnp.einsum("hqk,qhd->khd", grad_scores, query_view, preferred_element_type=f32)
            * score_scale
        )
        for slot, piece in enumerate((grad_query_view, grad_key_view, grad_value_view)):
            grad_qkv[slot].append(piece.reshape(seq_len, -1).astype(bf16))
    back_parts = []
    for i in range(image_count):
        partial = (
            times_transpose(grad_qkv[0][i], query_weight)
            + times_transpose(grad_qkv[1][i], key_weight)
            + times_transpose(grad_qkv[2][i], value_weight)
        )
        back_parts += [partial[s * rows : (s + 1) * rows] for s in range(share)]
    grad_ln_one = scatter_sum(back_parts, "tensor")
    context = jnp.concatenate(context_list, axis=0)
    cot_one = jnp.concatenate(cot_img, axis=0)
    ln_one_all = jnp.concatenate(ln_one_img, axis=0)
    grad_query_all, grad_key_all, grad_value_all = (jnp.concatenate(p, axis=0) for p in grad_qkv)
    grad_out = transpose_times(context, cot_one)
    grad_query = transpose_times(grad_query_all, ln_one_all)
    grad_key = transpose_times(grad_key_all, ln_one_all)
    grad_value = transpose_times(grad_value_all, ln_one_all)
    attn_grads = lax.psum(
        tuple(g.astype(bf16) for g in (grad_query, grad_key, grad_value, grad_out)), "dp"
    )
    grad_states, grad_gain_one, grad_bias_one = norm_one_back(grad_ln_one)
    grad_input = (grad_one + grad_states).astype(bf16)
    by_unit = lax.psum(
        (
            jnp.sum(grad_query_all.astype(f32), axis=0),
            jnp.sum(grad_value_all.astype(f32), axis=0),
        ),
        "dp",
    )
    summed = lax.psum(
        (
            grad_gain_one,
            grad_bias_one,
            grad_out_bias,
            grad_gain_two,
            grad_bias_two,
            grad_down_bias,
            squares_here,
            grad_up_bias_all,
        ),
        ("dp", "tensor"),
    )
    return (
        out_states,
        summed[6] / token_total,
        grad_input,
        summed[0],
        summed[1],
        attn_grads[0].T.astype(f32),
        by_unit[0],
        attn_grads[1].T.astype(f32),
        attn_grads[2].T.astype(f32),
        by_unit[1],
        attn_grads[3].astype(f32),
        summed[2],
        summed[3],
        summed[4],
        mlp_grads[1].T.astype(f32),
        jnp.dot((jnp.arange(tensor_size) == here).astype(f32)[None, :], summed[7], precision=lax.Precision.HIGHEST)[0],
        mlp_grads[0].astype(f32),
        summed[5],
    )


def solution(mesh):
    placed = (
        P(("dp", "tensor"), None),
        P(("dp", "tensor"), None),
        P("dp"),
        P(),
        P(),
        P(None, "tensor"),
        P("tensor"),
        P(None, "tensor"),
        P(None, "tensor"),
        P("tensor"),
        P("tensor", None),
        P(),
        P(),
        P(),
        P(None, "tensor"),
        P("tensor"),
        P("tensor", None),
        P(),
    )
    return jax.shard_map(
        per_device,
        mesh=mesh,
        in_specs=placed,
        out_specs=(
            P(("dp", "tensor"), None),
            P(),
            P(("dp", "tensor"), None),
            P(),
            P(),
            P(None, "tensor"),
            P("tensor"),
            P(None, "tensor"),
            P(None, "tensor"),
            P("tensor"),
            P("tensor", None),
            P(),
            P(),
            P(),
            P(None, "tensor"),
            P("tensor"),
            P("tensor", None),
            P(),
        ),
        check_vma=False,
    )
```
